32 devices in a mesh: aa: 8 (over y, x, core), col: 4 (over z).
Axes of the slice: x: 2, y: 2, z: 4, core: 2. Of those that a mesh axis runs over, the one named last changes fastest.
Arguments:
- fit_ac: float32 [512, 512, 2048], P('aa', 'col'), may hold values from -0.125 to 0.125
- fit_bd: float32 [2048, 1024], P(('aa', 'col')), may hold values from -6 to 6
- amplitudes: float32 [2, 32, 512, 256], P(None, 'aa', 'col'), may hold values from -0.046875 to 0.046875
Outputs:
- residual: float32 [2, 16, 512, 256], P(None, 'col', 'aa')
The draws below stay inside these ranges and needn't reach their ends.
All inputs are finite; a program needn't handle non-finite values.
Results may differ from the reference program's by a relative error of at most 0.0003.
Values sent between devices are 32-bit elements; how exact they have to be, the bound alone decides.
A program may use at most 192 MiB of HBM per device.

```python
import jax
import jax.numpy as jnp
from jax import lax

V = 512
NQ = 2048
KB = 2
NB = 16
ND = 32
P_SIZE = 256
N_AA = 8


def levels(own_key, extent, cuts, low, top_value):
    gain = 1.0
    for axis_at, parts in cuts:
        steps = jax.random.uniform(jax.random.fold_in(jax.random.fold_in(own_key, 6), axis_at), (parts,), jnp.float32, low / len(cuts), top_value / len(cuts))
        gain = gain * jnp.repeat(jnp.exp(steps), extent[axis_at] // parts).reshape((-1,) + (1,) * (len(extent) - 1 - axis_at))
    return gain


def normal_values(stream_key, extent, spread, most, cuts=(), held_as=jnp.bfloat16):
    factor_of = levels(stream_key, extent, cuts, -0.22, 0.18) if cuts else 1.0
    entries = jax.random.normal(stream_key, extent, jnp.float32) * spread * factor_of
    return jnp.minimum(jnp.maximum(entries, -most), most).astype(held_as)


def setup_inputs(seed: int = 0) -> dict:
    splits = jax.random.split(jax.random.key(seed), 4)
    return {
        "fit_ac": normal_values(splits[0], (V, V, NQ), NQ ** -0.5, 0.125, ((0, 8), (1, 4)), jnp.float32),
        "fit_bd": normal_values(splits[1], (NQ, KB * NB * ND), 1.0, 6.0, ((0, 32),), jnp.float32),
        "amplitudes": normal_values(splits[2], (KB, ND, V, P_SIZE), (V * ND) ** -0.5, 0.046875, ((1, 8), (2, 4)), jnp.float32),
    }


def reference(fit_ac, fit_bd, amplitudes):
    a_block = V // N_AA

    def one_block(index):
        start = (index * a_block).astype(jnp.int32)
        piece = lax.dynamic_slice_in_dim(fit_ac, start, a_block, 0)
        integrals = jnp.dot(piece.reshape(a_block * V, NQ), fit_bd, precision=lax.Precision.HIGHEST, preferred_element_type=jnp.float32)
        integrals = integrals.reshape(a_block, V, KB, NB, ND)
        return jnp.einsum("kdcp,ackbd->kbap", amplitudes, integrals, precision=lax.Precision.HIGHEST)

    pieces = lax.map(one_block, jnp.arange(V // a_block, dtype=jnp.int32))
    return pieces.transpose(1, 2, 0, 3, 4).reshape(KB, NB, V, P_SIZE)
```

```python
import functools

import jax
import jax.numpy as jnp
from jax import lax
from jax.experimental import pallas as pl
from jax.experimental.pallas import tpu as pltpu
from jax.sharding import PartitionSpec as P

F32 = jnp.float32
BF16 = jnp.bfloat16
F8 = jnp.float8_e4m3fn
NT = (((1,), (1,)), ((), ()))
MESH = pl.DeviceIdType.MESH
VMEM_LIMIT = 67_000_000

A_HI, A_LO, B_HI, B_LO = 2.0**11, 2.0**20, 2.0**5, 2.0**14
SCALE, UNDO = 2.0**25, 2.0**-25
LANES = 128
PARTS = 2


def split(value):
    high = value.astype(BF16)
    return high, value - high.astype(F32)


class Plan:
    def __init__(self, n_aa, n_col, fit_ac, fit_bd, amplitudes):
        self.n_aa, self.n_col = n_aa, n_col
        self.a_local, self.c_local, self.count_q = fit_ac.shape
        self.blocks, self.d_local, _, self.pairs = amplitudes.shape
        self.q_local, self.columns = fit_bd.shape
        self.d_size = self.d_local * n_aa
        self.b_size = self.columns // (self.blocks * self.d_size)
        self.b_out = self.b_size // n_col
        self.near = min(n_col, max(1, LANES // self.q_local))
        self.halves = n_col // self.near
        self.depth = self.near * self.q_local
        self.far = [1 << bit for bit in range(1, n_aa.bit_length() - 1)]
        self.orders = [self.far, self.far[::-1]]
        masks = [mask for mask in range(0, n_aa, 2)]
        ones = [m for m in masks if m.bit_count() == 1]
        more = [m for m in masks if m.bit_count() > 1]
        rest = range(1, self.halves)
        own = [(m, 0) for m in (0,)]
        self.phases = [own, [(m, 0) for m in ones], [(m, 0) for m in more] + [(0, r) for r in rest]]
        self.phases.append([(m, r) for r in rest for m in ones + more])
        self.phases = [[(m ^ core, r) for m, r in phase for core in (0, 1)] for phase in self.phases if phase]
        self.group = min(self.a_local, 16)
        self.rows = [8 if len(phase) <= 4 else 4 for phase in self.phases]
        self.waves = [[], [], []]
        for part, order in enumerate(self.orders):
            for mask in sorted(masks[1:], key=lambda m: m.bit_count()):
                stage = max(order.index(bit) for bit in self.far if bit & mask)
                wave = 2 if mask.bit_count() > 1 else (0 if stage == 0 else 1)
                self.waves[wave].append((part, mask, order[stage], order[stage + 1 :]))
        self.waves[2].sort(key=lambda one: one[1].bit_count())
        self.moves = PARTS * (n_aa // 2 - 1 + n_aa // 2)


class Exchange:
    def __init__(self, plan, source, target, send, recv, place):
        self.plan, self.source, self.target = plan, source, target
        self.send, self.recv, self.place, self.keys = send, recv, place, {}

    def copy(self, part, mask, bit):
        index = self.keys.setdefault((part, mask, bit), len(self.keys))
        aa, col = self.place
        return pltpu.make_async_remote_copy(
            src_ref=self.source(part, mask),
            dst_ref=self.target(part, mask),
            send_sem=self.send.at[index],
            recv_sem=self.recv.at[index],
            device_id=(aa ^ bit, col),
            device_id_type=MESH,
        )

    def own(self):
        for stage in range(len(self.plan.far)):
            for part, order in enumerate(self.plan.orders):
                self.copy(part, 0, order[stage]).start()
        for part in range(PARTS):
            self.copy(part, 0, 1).start()

    def wave(self, which):
        for part, mask, bit, later in self.plan.waves[which]:
            self.copy(part, mask ^ bit, bit).wait_recv()
            for further in later:
                self.copy(part, mask, further).start()
            self.copy(part, mask, 1).start()

    def core(self, mask):
        for part in range(PARTS):
            self.copy(part, mask ^ 1, 1).wait_recv()

    def finish(self):
        for key in list(self.keys):
            self.copy(*key).wait_send()


def kernel(
    plan, fit_ac, fit_bd, amplitudes, sums, bd_all, t_all,
    acc, high, low8, high8, t_high, t_low, blocks_a, stage, turned, t_stage, made, ready,
    a_sem, own_sem, stage_sem, t_sem, z_send, z_recv, x_send, x_recv, r_send, r_recv, r_own,
):
    aa, col = lax.axis_index("aa").astype(jnp.int32), lax.axis_index("col").astype(jnp.int32)
    n_col, n_aa = plan.n_col, plan.n_aa
    q_local, depth, d_local = plan.q_local, plan.depth, plan.d_local
    half = plan.columns // PARTS

    barrier = pltpu.get_barrier_semaphore()
    peers = [(aa, col ^ step) for step in range(1, n_col)] + [(aa ^ bit, col) for bit in [1] + plan.far]
    for peer in peers:
        pl.semaphore_signal(barrier, inc=1, device_id=peer, device_id_type=MESH)

    mine = pl.ds(pl.multiple_of((aa * n_col + col) * q_local, q_local), q_local)
    take = pltpu.make_async_copy(fit_bd, stage.at[0, pl.ds(0, q_local)], own_sem.at[0])
    take.start()
    keep = pltpu.make_async_copy(amplitudes, t_all.at[:, pl.ds(aa * d_local, d_local)], own_sem.at[1])
    keep.start()
    pl.semaphore_wait(barrier, len(peers))

    along = []
    for step in range(1, n_col):
        along.append(
            pltpu.make_async_remote_copy(
                src_ref=fit_bd,
                dst_ref=bd_all.at[mine],
                send_sem=z_send.at[step - 1],
                recv_sem=z_recv.at[step - 1],
                device_id=(aa, col ^ step),
                device_id_type=MESH,
            )
        )
        along[-1].start()
    take.wait()
    put = pltpu.make_async_copy(stage.at[0, pl.ds(0, q_local)], bd_all.at[mine], own_sem.at[0])
    put.start()

    def first_q(mask, rel):
        return pl.multiple_of(((aa ^ mask) * n_col + ((col // plan.near) ^ rel) * plan.near) * q_local, depth)

    def bd_piece(rel, part, mask):
        return bd_all.at[pl.ds(first_q(mask, rel), depth), pl.ds(part * half, half)]

    def t_piece(part, mask):
        return t_all.at[part, pl.ds((aa ^ mask) * d_local, d_local)]

    def t_source(part, mask):
        return amplitudes.at[part] if mask == 0 else t_piece(part, mask)

    place = (aa, col)
    exchanges = []
    for rel in range(plan.halves):
        piece = functools.partial(bd_piece, rel)
        exchanges.append(Exchange(plan, piece, piece, x_send.at[rel], x_recv.at[rel], place))
    exchange_t = Exchange(plan, t_source, t_piece, x_send.at[plan.halves], x_recv.at[plan.halves], place)

    def begin_half(rel):
        for step in range(max(1, rel * plan.near), (rel + 1) * plan.near):
            along[step - 1].wait_recv()
        if rel == 0:
            put.wait()
        exchanges[rel].own()

    last = len(plan.phases) - 1
    events = [(0, 2, lambda: exchanges[0].wave(0))]
    if plan.halves > 1:
        for rel in range(1, plan.halves):
            events.append((0, 6, functools.partial(begin_half, rel)))
    events.append((1, -1, lambda: exchanges[0].wave(1)))
    events.append((1, 0, lambda: exchanges[0].wave(2)))
    for rel in range(1, plan.halves):
        events.append((1, 2, functools.partial(exchanges[rel].wave, 0)))
        events.append((1, 4, functools.partial(exchanges[rel].wave, 1)))
    events.append((1, 4, exchange_t.own))
    for rel in range(1, plan.halves):
        events.append((1, 7, functools.partial(exchanges[rel].wave, 2)))
    events.append((2, 3, lambda: exchange_t.wave(0)))
    events.append((2, 6, lambda: exchange_t.wave(1)))

    def run_events(phase, at):
        for when, step, act in events:
            if when == phase and step == at:
                act()

    def loads(phase, index, slot):
        rows = plan.rows[phase]
        found = []
        for at, (mask, rel) in enumerate(plan.phases[phase]):
            found.append(
                pltpu.make_async_copy(
                    fit_ac.at[pl.ds(index * rows, rows), :, pl.ds(first_q(mask, rel), depth)],
                    blocks_a.at[slot, at % 4, pl.ds(at // 4 * rows, rows)],
                    a_sem.at[slot, at],
                )
            )
        return found

    def fetch(phase, index, slot):
        for one in loads(phase, index, slot):
            one.start()

    def prepare(phase, base):
        pieces = plan.phases[phase]
        for mask, rel in pieces:
            if mask & 1:
                exchanges[rel].core(mask)
        starts = [first_q(mask, rel) for mask, rel in pieces]

        def source(at):
            row = starts[0]
            for one in range(1, len(starts)):
                row = jnp.where(at == one, starts[one], row)
            slot = lax.rem(at, 2)
            row = pl.multiple_of(row, depth)
            return pltpu.make_async_copy(bd_all.at[pl.ds(row, depth)], stage.at[slot], stage_sem.at[slot])

        source(jnp.int32(0)).start()

        @pl.loop(0, len(pieces))
        def _(at):
            @pl.when(at + 1 < len(pieces))
            def _():
                source(at + 1).start()

            source(at).wait()
            turned[...] = stage[lax.rem(at, 2)].T
            lanes = pl.ds(pl.multiple_of(base + at * depth, depth), depth)
            for k in range(plan.blocks):
                for d in range(0, plan.d_size, 2):
                    first = k * plan.b_size * plan.d_size + d
                    value = jnp.concatenate(
                        [turned[pl.ds(first + one, plan.b_size, stride=plan.d_size), :] for one in range(2)], axis=0
                    )
                    top, rest = split(value)
                    to = (pl.ds((k * plan.d_size + d) * plan.b_size, 2 * plan.b_size), lanes)
                    high[to] = (top.astype(F32) * SCALE).astype(BF16)
                    low8[to] = (rest * B_LO).astype(F8)
                    high8[to] = (value * B_HI).astype(F8)

    dot = functools.partial(lax.dot_general, dimension_numbers=NT, preferred_element_type=F32)

    def multiply(phase, base, index):
        pieces, rows = plan.phases[phase], plan.rows[phase]
        slot = lax.rem(index, 2)
        for one in loads(phase, index, slot):
            one.wait()
        parts = [
            blocks_a[slot, at % 4, at // 4 * rows : at // 4 * rows + rows].reshape(rows * plan.c_local, depth)
            for at in range(len(pieces))
        ]
        value = jnp.concatenate(parts, axis=1)
        top, rest = split(value)
        lanes = slice(base, base + depth * len(pieces))
        made_here = dot(high[:, lanes], top)
        made_here += dot(low8[:, lanes], (value * A_HI).astype(F8))
        made_here += dot(high8[:, lanes], (rest * A_LO).astype(F8))
        count = plan.blocks * plan.d_size
        for row in range(rows):
            one = made_here[:, row * plan.c_local : (row + 1) * plan.c_local]
            one = one.reshape(count, plan.b_size, plan.c_local)
            at = index * rows + row
            if phase == 0:
                acc[:, at] = one
            else:
                acc[:, at] += one

    begin_half(0)
    fetch(0, 0, 0)
    base = 0
    for phase in range(last):
        run_events(phase, -1)
        prepare(phase, base)
        steps = plan.a_local // plan.rows[phase]

        @pl.loop(0, steps)
        def _(index, phase=phase, base=base, steps=steps):
            @pl.when(index + 1 < steps)
            def _():
                fetch(phase, index + 1, lax.rem(index + 1, 2))

            @pl.when(index + 1 == steps)
            def _():
                fetch(phase + 1, 0, steps % 2)

            for at in range(steps):
                if any(when == phase and step == at for when, step, _ in events):
                    pl.when(index == at)(functools.partial(run_events, phase, at))
            multiply(phase, base, index)

        for at in range(steps, 8):
            run_events(phase, at)
        base += depth * len(plan.phases[phase])

    for at in range(-1, 8):
        run_events(last, at)
    prepare(last, base)
    span = d_local * plan.c_local

    def prepare_t():
        if last < 2:
            exchange_t.wave(0)
            exchange_t.wave(1)
        exchange_t.wave(2)
        keep.wait()
        for mask in range(1, n_aa, 2):
            exchange_t.core(mask)
        count = plan.blocks * n_aa

        def source(at):
            slot = lax.rem(at, 2)
            src = t_all.at[at // n_aa, pl.ds(lax.rem(at, n_aa) * d_local, d_local)]
            return pltpu.make_async_copy(src, t_stage.at[slot], t_sem.at[slot])

        source(jnp.int32(0)).start()

        @pl.loop(0, count)
        def _(at):
            @pl.when(at + 1 < count)
            def _():
                source(at + 1).start()

            source(at).wait()
            value = t_stage[lax.rem(at, 2)].reshape(span, plan.pairs) * UNDO
            top, rest = split(value)
            to = (at // n_aa, pl.ds(pl.multiple_of(lax.rem(at, n_aa) * span, span), span))
            t_high[to] = top
            t_low[to] = rest.astype(BF16)

    group, rows = plan.group, plan.rows[last]
    groups, inner = plan.a_local // group, plan.group // rows
    plain = functools.partial(jnp.dot, preferred_element_type=F32)
    wide = 8 if plan.c_local % LANES == 0 else 1

    def ladder(k, which):
        total = None
        for d in range(0, plan.d_size, wide):
            parts = []
            for one in range(d, d + wide):
                part = acc[k * plan.d_size + one, pl.ds(which * group, group)]
                parts.append(part.reshape(group * plan.b_size, plan.c_local))
            x_high, x_low = split(jnp.concatenate(parts, axis=1) if wide > 1 else parts[0])
            at = slice(d * plan.c_local, (d + wide) * plan.c_local)
            t_top, t_rest = t_high[k, at], t_low[k, at]
            term = plain(x_high, t_top) + plain(x_low.astype(BF16), t_top) + plain(x_high, t_rest)
            total = term if total is None else total + term
        return total

    def away(which, step):
        slot = lax.rem(which, 2)
        to = col ^ step
        src = ready.at[slot, :, pl.ds(to * plan.b_out, plan.b_out)]
        dst = sums.at[step, :, :, pl.ds(which * group, group)]
        if step == 0:
            return pltpu.make_async_copy(src, dst, r_own.at[slot])
        return pltpu.make_async_remote_copy(
            src_ref=src,
            dst_ref=dst,
            send_sem=r_send.at[slot, step - 1],
            recv_sem=r_recv.at[which, step - 1],
            device_id=(aa, to),
            device_id_type=MESH,
        )

    def left(which):
        away(which, 0).wait()
        for step in range(1, n_col):
            away(which, step).wait_send()

    steps = groups * inner

    @pl.loop(0, groups)
    def _(which):
        @pl.loop(0, inner)
        def _(sub):
            index = which * inner + sub

            @pl.when(index + 1 < steps)
            def _():
                fetch(last, index + 1, lax.rem(index + 1, 2))

            multiply(last, base, index)

        pl.when(which == 0)(prepare_t)

        @pl.when(which >= 2)
        def _():
            left(which - 2)

        slot = lax.rem(which, 2)

        @pl.loop(0, plan.blocks)
        def _(k):
            total = ladder(k, which)
            for at in range(0, plan.pairs, LANES):
                made[...] = total[:, at : at + LANES]
                for b in range(plan.b_size):
                    ready[slot, k, b, :, at : at + LANES] = made[pl.ds(b, group, stride=plan.b_size), :]

        for step in range(1, n_col):
            away(which, step).start()
        away(which, 0).start()

    for which in range(max(0, groups - 2), groups):
        left(jnp.int32(which))
    for one in along:
        one.wait_send()
    for one in exchanges + [exchange_t]:
        one.finish()
    for which in range(groups):
        for step in range(1, n_col):
            away(jnp.int32(which), step).wait_recv()


def shards(n_aa, n_col, fit_ac, fit_bd, amplitudes):
    plan = Plan(n_aa, n_col, fit_ac, fit_bd, amplitudes)
    columns, count_q, c_local, pairs = plan.columns, plan.count_q, plan.c_local, plan.pairs
    dma, any_ = pltpu.SemaphoreType.DMA, pl.BlockSpec(memory_space=pl.ANY)
    groups = plan.a_local // plan.group
    most = max(len(phase) for phase in plan.phases)
    sums, _, _ = pl.pallas_call(
        functools.partial(kernel, plan),
        in_specs=[any_] * 3,
        out_specs=[any_] * 3,
        out_shape=[
            jax.ShapeDtypeStruct((n_col, plan.blocks, plan.b_out, plan.a_local, pairs), F32),
            jax.ShapeDtypeStruct((count_q, columns), F32),
            jax.ShapeDtypeStruct((plan.blocks, plan.d_size, c_local, pairs), F32),
        ],
        scratch_shapes=[
            pltpu.VMEM((plan.blocks * plan.d_size, plan.a_local, plan.b_size, c_local), F32),
            pltpu.VMEM((columns, count_q), BF16),
            pltpu.VMEM((columns, count_q), F8),
            pltpu.VMEM((columns, count_q), F8),
            pltpu.VMEM((plan.blocks, plan.d_size * c_local, pairs), BF16),
            pltpu.VMEM((plan.blocks, plan.d_size * c_local, pairs), BF16),
            pltpu.VMEM((2, 4, 8, c_local, plan.depth), F32),
            pltpu.VMEM((2, plan.depth, columns), F32),
            pltpu.VMEM((columns, plan.depth), F32),
            pltpu.VMEM((2, plan.d_local, c_local, pairs), F32),
            pltpu.VMEM((plan.group * plan.b_size, LANES), F32),
            pltpu.VMEM((2, plan.blocks, plan.b_size, plan.group, pairs), F32),
            dma((2, most)),
            dma((2,)),
            dma((2,)),
            dma((2,)),
            dma((n_col - 1,)),
            dma((n_col - 1,)),
            dma((plan.halves + 1, plan.moves)),
            dma((plan.halves + 1, plan.moves)),
            dma((2, n_col - 1)),
            dma((groups, n_col - 1)),
            dma((2,)),
        ],
        compiler_params=pltpu.CompilerParams(vmem_limit_bytes=VMEM_LIMIT, collective_id=0, has_side_effects=True),
    )(fit_ac, fit_bd, amplitudes)
    return sums.sum(axis=0)


def solution(mesh):
    placed = (P("aa", "col", None), P(("aa", "col"), None), P(None, "aa", "col", None))
    body = functools.partial(shards, mesh.shape["aa"], mesh.shape["col"])
    return jax.shard_map(
        body, mesh=mesh, in_specs=placed, out_specs=P(None, "col", "aa", None), check_vma=False
    )
```

```python
import functools

import jax
import jax.numpy as jnp
from jax import lax
from jax.experimental import pallas as pl
from jax.experimental.pallas import tpu as pltpu
from jax.sharding import PartitionSpec as P

F32 = jnp.float32
BF16 = jnp.bfloat16
F8 = jnp.float8_e4m3fn
NT = (((1,), (1,)), ((), ()))
MESH = pl.DeviceIdType.MESH
VMEM_LIMIT = 67_000_000

A_HI, A_LO, B_HI, B_LO = 2.0**11, 2.0**20, 2.0**5, 2.0**14
SCALE, UNDO = 2.0**25, 2.0**-25
LANES = 128
PARTS = 2


def split(value):
    high = value.astype(BF16)
    return high, value - high.astype(F32)


class Plan:
    def __init__(self, n_aa, n_col, fit_ac, fit_bd, amplitudes):
        self.n_aa, self.n_col = n_aa, n_col
        self.a_local, self.c_local, self.count_q = fit_ac.shape
        self.blocks, self.d_local, _, self.pairs = amplitudes.shape
        self.q_local, self.columns = fit_bd.shape
        self.d_size = self.d_local * n_aa
        self.b_size = self.columns // (self.blocks * self.d_size)
        self.b_out = self.b_size // n_col
        self.near = min(n_col, max(1, LANES // self.q_local))
        self.halves = n_col // self.near
        self.depth = self.near * self.q_local
        self.far = [1 << bit for bit in range(1, n_aa.bit_length() - 1)]
        self.orders = [self.far, self.far[::-1]]
        masks = [mask for mask in range(0, n_aa, 2)]
        ones = [m for m in masks if m.bit_count() == 1]
        more = [m for m in masks if m.bit_count() > 1]
        rest = range(1, self.halves)
        own = [(m, 0) for m in (0,)]
        self.phases = [own, [(m, 0) for m in ones], [(m, 0) for m in more] + [(0, r) for r in rest]]
        self.phases.append([(m, r) for r in rest for m in ones + more])
        self.phases = [[(m ^ core, r) for core in (0, 1) for m, r in phase] for phase in self.phases if phase]
        self.group = min(self.a_local, 16)
        self.tail = self.group // 2
        self.rows = [8 if len(phase) <= 4 else 4 for phase in self.phases]
        self.waves = [[], [], []]
        for part, order in enumerate(self.orders):
            for mask in sorted(masks[1:], key=lambda m: m.bit_count()):
                stage = max(order.index(bit) for bit in self.far if bit & mask)
                wave = 2 if mask.bit_count() > 1 else (0 if stage == 0 else 1)
                self.waves[wave].append((part, mask, order[stage], order[stage + 1 :]))
        self.waves[2].sort(key=lambda one: one[1].bit_count())
        self.t_each = -(-n_aa * self.rows[-1] // self.group)
        self.moves = PARTS * (n_aa // 2 - 1 + n_aa // 2)


class Exchange:
    def __init__(self, plan, source, target, send, recv, place):
        self.plan, self.source, self.target = plan, source, target
        self.send, self.recv, self.place, self.keys = send, recv, place, {}

    def copy(self, part, mask, bit):
        index = self.keys.setdefault((part, mask, bit), len(self.keys))
        aa, col = self.place
        return pltpu.make_async_remote_copy(
            src_ref=self.source(part, mask),
            dst_ref=self.target(part, mask),
            send_sem=self.send.at[index],
            recv_sem=self.recv.at[index],
            device_id=(aa ^ bit, col),
            device_id_type=MESH,
        )

    def own(self):
        for stage in range(len(self.plan.far)):
            for part, order in enumerate(self.plan.orders):
                self.copy(part, 0, order[stage]).start()
        for part in range(PARTS):
            self.copy(part, 0, 1).start()

    def wave(self, which):
        for part, mask, bit, later in self.plan.waves[which]:
            self.copy(part, mask ^ bit, bit).wait_recv()
            for further in later:
                self.copy(part, mask, further).start()
            self.copy(part, mask, 1).start()

    def core(self, mask):
        for part in range(PARTS):
            self.copy(part, mask ^ 1, 1).wait_recv()

    def finish(self):
        for key in list(self.keys):
            self.copy(*key).wait_send()


def kernel(plan, fit_ac, fit_bd, amplitudes, sums, bd_all, t_all, *refs):
    count = len(plan.phases)
    highs, lows8, highs8 = refs[:count], refs[count : 2 * count], refs[2 * count : 3 * count]
    acc, t_high, t_low, blocks_a, stage, turned, t_stage, made, ready = refs[3 * count : 3 * count + 9]
    a_sem, own_sem, stage_sem, t_sem, z_send, z_recv, x_send, x_recv, r_send, r_recv, r_own = refs[3 * count + 9 :]
    aa, col = lax.axis_index("aa").astype(jnp.int32), lax.axis_index("col").astype(jnp.int32)
    n_col, n_aa = plan.n_col, plan.n_aa
    q_local, depth, d_local = plan.q_local, plan.depth, plan.d_local
    half = plan.columns // PARTS

    barrier = pltpu.get_barrier_semaphore()
    peers = [(aa, col ^ step) for step in range(1, n_col)] + [(aa ^ bit, col) for bit in [1] + plan.far]
    for peer in peers:
        pl.semaphore_signal(barrier, inc=1, device_id=peer, device_id_type=MESH)

    mine = pl.ds(pl.multiple_of((aa * n_col + col) * q_local, q_local), q_local)
    take = pltpu.make_async_copy(fit_bd, stage.at[0, pl.ds(0, q_local)], own_sem.at[0])
    take.start()
    keep = pltpu.make_async_copy(amplitudes, t_all.at[:, pl.ds(aa * d_local, d_local)], own_sem.at[1])
    keep.start()
    pl.semaphore_wait(barrier, len(peers))

    along = []
    for step in range(1, n_col):
        along.append(
            pltpu.make_async_remote_copy(
                src_ref=fit_bd,
                dst_ref=bd_all.at[mine],
                send_sem=z_send.at[step - 1],
                recv_sem=z_recv.at[step - 1],
                device_id=(aa, col ^ step),
                device_id_type=MESH,
            )
        )
        if step < plan.near:
            along[-1].start()
    take.wait()
    put = pltpu.make_async_copy(stage.at[0, pl.ds(0, q_local)], bd_all.at[mine], own_sem.at[0])
    put.start()

    def first_q(mask, rel):
        return pl.multiple_of(((aa ^ mask) * n_col + ((col // plan.near) ^ rel) * plan.near) * q_local, depth)

    def bd_piece(rel, part, mask):
        return bd_all.at[pl.ds(first_q(mask, rel), depth), pl.ds(part * half, half)]

    def t_piece(part, mask):
        return t_all.at[part, pl.ds((aa ^ mask) * d_local, d_local)]

    def t_source(part, mask):
        return amplitudes.at[part] if mask == 0 else t_piece(part, mask)

    place = (aa, col)
    exchanges = []
    for rel in range(plan.halves):
        piece = functools.partial(bd_piece, rel)
        exchanges.append(Exchange(plan, piece, piece, x_send.at[rel], x_recv.at[rel], place))
    exchange_t = Exchange(plan, t_source, t_piece, x_send.at[plan.halves], x_recv.at[plan.halves], place)

    def begin_half(rel):
        for step in range(max(1, rel * plan.near), (rel + 1) * plan.near):
            along[step - 1].wait_recv()
        if rel == 0:
            for step in range(plan.near, n_col):
                along[step - 1].start()
            put.wait()
        exchanges[rel].own()

    last = len(plan.phases) - 1
    events = [(0, 4, lambda: exchanges[0].wave(0)), (0, 7, exchange_t.own)]
    events.append((1, -1, lambda: exchanges[0].wave(1)))
    events.append((1, 0, lambda: exchanges[0].wave(2)))
    for rel in range(1, plan.halves):
        events.append((1, 2, functools.partial(begin_half, rel)))
        events.append((1, 5, functools.partial(exchanges[rel].wave, 0)))
    events.append((1, 7, lambda: exchange_t.wave(0)))
    for rel in range(1, plan.halves):
        events.append((2, 0, functools.partial(exchanges[rel].wave, 1)))
        events.append((2, 2, functools.partial(exchanges[rel].wave, 2)))
    events.append((2, 4, lambda: exchange_t.wave(1)))

    def run_events(phase, at):
        for when, step, act in events:
            if when == phase and step == at:
                act()

    def loads(phase, index, slot):
        rows = plan.rows[phase]
        found = []
        for at, (mask, rel) in enumerate(plan.phases[phase]):
            found.append(
                pltpu.make_async_copy(
                    fit_ac.at[pl.ds(index * rows, rows), :, pl.ds(first_q(mask, rel), depth)],
                    blocks_a.at[slot, at % 4, pl.ds(at // 4 * rows, rows)],
                    a_sem.at[slot, at],
                )
            )
        return found

    def fetch(phase, index, slot):
        for one in loads(phase, index, slot):
            one.start()

    def bring(phase, at):
        pieces = plan.phases[phase]
        row = jnp.int32(0)
        for one, (mask, rel) in enumerate(pieces):
            row = jnp.where(at == one, first_q(mask, rel), row)
        slot = lax.rem(at, 2)
        return pltpu.make_async_copy(
            bd_all.at[pl.ds(pl.multiple_of(row, depth), depth)], stage.at[slot], stage_sem.at[slot]
        )

    def start_bring(phase, at):
        pieces = plan.phases[phase]
        for one, (mask, rel) in enumerate(pieces):
            if mask & 1:
                pl.when(at == one)(functools.partial(exchanges[rel].core, mask))

        @pl.when(at < len(pieces))
        def _():
            bring(phase, at).start()

    def arrange(phase, at):
        turned[...] = stage[lax.rem(at, 2)].T
        lanes = pl.ds(pl.multiple_of(at * depth, depth), depth)
        for k in range(plan.blocks):
            for d in range(0, plan.d_size, 2):
                first = k * plan.b_size * plan.d_size + d
                value = jnp.concatenate(
                    [turned[pl.ds(first + one, plan.b_size, stride=plan.d_size), :] for one in range(2)], axis=0
                )
                top, rest = split(value)
                to = (pl.ds((k * plan.d_size + d) * plan.b_size, 2 * plan.b_size), lanes)
                highs[phase][to] = (top.astype(F32) * SCALE).astype(BF16)
                lows8[phase][to] = (rest * B_LO).astype(F8)
                highs8[phase][to] = (value * B_HI).astype(F8)

    def prepare(phase):
        start_bring(phase, jnp.int32(0))
        start_bring(phase, jnp.int32(1))

        @pl.loop(0, len(plan.phases[phase]))
        def _(at):
            bring(phase, at).wait()
            arrange(phase, at)
            start_bring(phase, at + 2)

    dot = functools.partial(lax.dot_general, dimension_numbers=NT, preferred_element_type=F32)

    def multiply(phase, index):
        pieces, rows = plan.phases[phase], plan.rows[phase]
        slot = lax.rem(index, 2)
        for one in loads(phase, index, slot):
            one.wait()
        parts = [
            blocks_a[slot, at % 4, at // 4 * rows : at // 4 * rows + rows].reshape(rows * plan.c_local, depth)
            for at in range(len(pieces))
        ]
        value = jnp.concatenate(parts, axis=1)
        top, rest = split(value)
        made_here = dot(highs[phase][...], top)
        made_here += dot(lows8[phase][...], (value * A_HI).astype(F8))
        made_here += dot(highs8[phase][...], (rest * A_LO).astype(F8))
        count = plan.blocks * plan.d_size
        for row in range(rows):
            one = made_here[:, row * plan.c_local : (row + 1) * plan.c_local]
            one = one.reshape(count, plan.b_size, plan.c_local)
            at = index * rows + row
            if phase == 0:
                acc[:, at] = one
            else:
                acc[:, at] += one

    begin_half(0)
    fetch(0, 0, 0)
    prepared = False
    for phase in range(last):
        run_events(phase, -1)
        if not prepared:
            prepare(phase)
        steps, ahead = plan.a_local // plan.rows[phase], len(plan.phases[phase + 1])
        prepared = phase > 0 and ahead < steps
        plain_steps = steps - ahead if prepared else steps

        def before(index, low, high, phase=phase, steps=steps):
            @pl.when(index + 1 < steps)
            def _():
                fetch(phase, index + 1, lax.rem(index + 1, 2))

            @pl.when(index + 1 == steps)
            def _():
                fetch(phase + 1, 0, steps % 2)

            for at in range(low, high):
                if any(when == phase and step == at for when, step, _ in events):
                    pl.when(index == at)(functools.partial(run_events, phase, at))

        @pl.loop(0, plain_steps)
        def _(index, phase=phase, before=before, plain_steps=plain_steps):
            before(index, 0, plain_steps)
            multiply(phase, index)

        if prepared:
            start_bring(phase + 1, jnp.int32(0))

            @pl.loop(plain_steps, steps)
            def _(index, phase=phase, before=before, plain_steps=plain_steps, steps=steps):
                before(index, plain_steps, steps)
                at = index - plain_steps
                bring(phase + 1, at).wait()
                start_bring(phase + 1, at + 1)
                multiply(phase, index)
                arrange(phase + 1, at)

        for at in range(steps, 8):
            run_events(phase, at)

    for at in range(-1, 8):
        run_events(last, at)
    if not prepared:
        prepare(last)
    span = d_local * plan.c_local

    each = plan.t_each

    def t_copy(k, mask):
        slot = lax.rem(mask, 2 * each)
        src = t_all.at[k, pl.ds((aa ^ mask) * d_local, d_local)]
        return pltpu.make_async_copy(src, t_stage.at[slot], t_sem.at[slot])

    def t_arrange(k, mask):
        value = t_stage[lax.rem(mask, 2 * each)].reshape(span, plan.pairs) * UNDO
        top, rest = split(value)
        to = (k, pl.ds(pl.multiple_of((aa ^ mask) * span, span), span))
        t_high[to] = top
        t_low[to] = rest.astype(BF16)

    def t_begin(k, at):
        for one in range(each):
            t_copy(k, at * each + one).start()

    def t_end(k, at):
        for one in range(each):
            t_copy(k, at * each + one).wait()

    def t_work(k, at):
        for one in range(each):
            t_arrange(k, at * each + one)

    def t_gather(masks):
        for mask in masks:
            if mask & 1:
                exchange_t.core(mask)

    group, rows = plan.group, plan.rows[last]
    inner = group // rows
    plain = functools.partial(jnp.dot, preferred_element_type=F32)
    wide = 8 if plan.c_local % LANES == 0 else 1

    def ladder(k, start, size):
        total = None
        for d in range(0, plan.d_size, wide):
            parts = []
            for one in range(d, d + wide):
                part = acc[k * plan.d_size + one, pl.ds(start, size)]
                parts.append(part.reshape(size * plan.b_size, plan.c_local))
            x_high, x_low = split(jnp.concatenate(parts, axis=1) if wide > 1 else parts[0])
            at = slice(d * plan.c_local, (d + wide) * plan.c_local)
            t_top, t_rest = t_high[k, at], t_low[k, at]
            term = plain(x_high, t_top) + plain(x_low.astype(BF16), t_top) + plain(x_high, t_rest)
            total = term if total is None else total + term
        return total

    def away(start, size, number, step):
        to = col ^ step
        slot = lax.rem(number, 2)
        src = ready.at[slot, :, pl.ds(to * plan.b_out, plan.b_out), pl.ds(0, size)]
        dst = sums.at[step, :, :, pl.ds(start, size)]
        if step == 0:
            return pltpu.make_async_copy(src, dst, r_own.at[number])
        return pltpu.make_async_remote_copy(
            src_ref=src,
            dst_ref=dst,
            send_sem=r_send.at[number, step - 1],
            recv_sem=r_recv.at[number, step - 1],
            device_id=(aa, to),
            device_id_type=MESH,
        )

    total_steps = plan.a_local // rows

    def contract(index):
        @pl.when(index + 1 < total_steps)
        def _():
            fetch(last, index + 1, lax.rem(index + 1, 2))

        multiply(last, index)

    def left(start, size, number):
        away(start, size, number, 0).wait()
        for step in range(1, n_col):
            away(start, size, number, step).wait_send()

    def finish(start, size, number):
        slot = lax.rem(number, 2)

        @pl.loop(0, plan.blocks)
        def _(k):
            total = ladder(k, start, size)
            for at in range(0, plan.pairs, LANES):
                made[0 : size * plan.b_size] = total[:, at : at + LANES]
                for b in range(plan.b_size):
                    ready[slot, k, b, 0:size, at : at + LANES] = made[pl.ds(b, size, stride=plan.b_size), :]

        for step in range(1, n_col):
            away(start, size, number, step).start()
        away(start, size, number, 0).start()

    if last < 2:
        exchange_t.wave(0)
        exchange_t.wave(1)
    keep.wait()
    early = each * (inner - 1)
    late = not any((mask & ~1).bit_count() > 1 for mask in range(early))
    if not late:
        exchange_t.wave(2)
        early = n_aa
    t_gather(range(early))
    t_begin(0, 0)

    @pl.loop(0, inner)
    def _(index):
        if late:

            @pl.when(index == inner - 2)
            def _():
                exchange_t.wave(2)
                t_gather(range(early, n_aa))

        @pl.when(index + 1 < inner)
        def _():
            t_begin(0, index + 1)

        t_end(0, index)

        @pl.when(index + 1 < total_steps)
        def _():
            fetch(last, index + 1, lax.rem(index + 1, 2))

        multiply(last, index)
        t_work(0, index)

    t_begin(1, 0)

    @pl.loop(0, inner)
    def _(index):
        @pl.when(index + 1 < inner)
        def _():
            t_begin(1, index + 1)

        t_end(1, index)
        t_work(1, index)

    bulk = plan.a_local // group - 1

    @pl.loop(0, bulk)
    def _(which):
        @pl.when(which > 0)
        def _():
            @pl.loop(0, inner)
            def _(sub):
                contract(which * inner + sub)

        @pl.when(which >= 2)
        def _():
            left(pl.multiple_of((which - 2) * group, group), group, which - 2)

        finish(pl.multiple_of(which * group, group), group, which)

    tail, tail_inner = plan.tail, plan.tail // rows
    sent = [(which * group, group, jnp.int32(which)) for which in range(bulk)]
    sent += [(bulk * group + at * tail, tail, jnp.int32(bulk + at)) for at in range(2)]
    for at in range(2):

        @pl.loop(0, tail_inner)
        def _(sub, at=at):
            contract(bulk * inner + at * tail_inner + sub)

        if bulk + at >= 2:
            left(*sent[bulk + at - 2])
        finish(*sent[bulk + at])

    for one in sent[-2:]:
        left(*one)
    for one in along:
        one.wait_send()
    for one in exchanges + [exchange_t]:
        one.finish()
    for start, size, number in sent:
        for step in range(1, n_col):
            away(start, size, number, step).wait_recv()


def shards(n_aa, n_col, fit_ac, fit_bd, amplitudes):
    plan = Plan(n_aa, n_col, fit_ac, fit_bd, amplitudes)
    columns, count_q, c_local, pairs = plan.columns, plan.count_q, plan.c_local, plan.pairs
    dma, any_ = pltpu.SemaphoreType.DMA, pl.BlockSpec(memory_space=pl.ANY)
    sends = plan.a_local // plan.group + 1
    widths = [plan.depth * len(phase) for phase in plan.phases]
    most = max(len(phase) for phase in plan.phases)
    sums, _, _ = pl.pallas_call(
        functools.partial(kernel, plan),
        in_specs=[any_] * 3,
        out_specs=[any_] * 3,
        out_shape=[
            jax.ShapeDtypeStruct((n_col, plan.blocks, plan.b_out, plan.a_local, pairs), F32),
            jax.ShapeDtypeStruct((count_q, columns), F32),
            jax.ShapeDtypeStruct((plan.blocks, plan.d_size, c_local, pairs), F32),
        ],
        scratch_shapes=[pltpu.VMEM((columns, width), BF16) for width in widths]
        + [pltpu.VMEM((columns, width), F8) for width in widths * 2]
        + [
            pltpu.VMEM((plan.blocks * plan.d_size, plan.a_local, plan.b_size, c_local), F32),
            pltpu.VMEM((plan.blocks, plan.d_size * c_local, pairs), BF16),
            pltpu.VMEM((plan.blocks, plan.d_size * c_local, pairs), BF16),
            pltpu.VMEM((2, 4, 8, c_local, plan.depth), F32),
            pltpu.VMEM((2, plan.depth, columns), F32),
            pltpu.VMEM((columns, plan.depth), F32),
            pltpu.VMEM((2 * plan.t_each, plan.d_local, c_local, pairs), F32),
            pltpu.VMEM((plan.group * plan.b_size, LANES), F32),
            pltpu.VMEM((2, plan.blocks, plan.b_size, plan.group, pairs), F32),
            dma((2, most)),
            dma((2,)),
            dma((2,)),
            dma((2 * plan.t_each,)),
            dma((n_col - 1,)),
            dma((n_col - 1,)),
            dma((plan.halves + 1, plan.moves)),
            dma((plan.halves + 1, plan.moves)),
            dma((sends, n_col - 1)),
            dma((sends, n_col - 1)),
            dma((sends,)),
        ],
        compiler_params=pltpu.CompilerParams(vmem_limit_bytes=VMEM_LIMIT, collective_id=0, has_side_effects=True),
    )(fit_ac, fit_bd, amplitudes)
    return sums.sum(axis=0)


def solution(mesh):
    placed = (P("aa", "col", None), P(("aa", "col"), None), P(None, "aa", "col", None))
    body = functools.partial(shards, mesh.shape["aa"], mesh.shape["col"])
    return jax.shard_map(
        body, mesh=mesh, in_specs=placed, out_specs=P(None, "col", "aa", None), check_vma=False
    )
```

```python
import functools

import jax
import jax.numpy as jnp
from jax import lax
from jax.experimental import pallas as pl
from jax.experimental.pallas import tpu as pltpu
from jax.sharding import PartitionSpec as P

F32 = jnp.float32
BF16 = jnp.bfloat16
F8 = jnp.float8_e4m3fn
NT = (((1,), (1,)), ((), ()))
MESH = pl.DeviceIdType.MESH
VMEM_LIMIT = 67_000_000

A_HI, A_LO, B_HI, B_LO = 2.0**11, 2.0**20, 2.0**5, 2.0**14
SCALE, UNDO = 2.0**25, 2.0**-25
LANES = 128
PARTS = 2


def split(value):
    high = value.astype(BF16)
    return high, value - high.astype(F32)


class Plan:
    def __init__(self, n_aa, n_col, fit_ac, fit_bd, amplitudes):
        self.n_aa, self.n_col = n_aa, n_col
        self.a_local, self.c_local, self.count_q = fit_ac.shape
        self.blocks, self.d_local, _, self.pairs = amplitudes.shape
        self.q_local, self.columns = fit_bd.shape
        self.d_size = self.d_local * n_aa
        self.b_size = self.columns // (self.blocks * self.d_size)
        self.b_out = self.b_size // n_col
        self.near = min(n_col, max(1, LANES // self.q_local))
        self.halves = n_col // self.near
        self.depth = self.near * self.q_local
        self.far = [1 << bit for bit in range(1, n_aa.bit_length() - 1)]
        self.orders = [self.far, self.far[::-1]]
        masks = [mask for mask in range(0, n_aa, 2)]
        ones = [m for m in masks if m.bit_count() == 1]
        more = [m for m in masks if m.bit_count() > 1]
        rest = range(1, self.halves)
        own = [(m, 0) for m in (0,)]
        self.phases = [own, [(m, 0) for m in ones], [(m, 0) for m in more] + [(0, r) for r in rest]]
        self.phases.append([(m, r) for r in rest for m in ones + more])
        self.phases = [[(m ^ core, r) for core in (0, 1) for m, r in phase] for phase in self.phases if phase]
        self.group = min(self.a_local, 16)
        self.tail = self.group // 2
        self.rows = [8 if len(phase) <= 4 else 4 for phase in self.phases]
        self.waves = [[], [], []]
        for part, order in enumerate(self.orders):
            for mask in sorted(masks[1:], key=lambda m: m.bit_count()):
                stage = max(order.index(bit) for bit in self.far if bit & mask)
                wave = 2 if mask.bit_count() > 1 else (0 if stage == 0 else 1)
                self.waves[wave].append((part, mask, order[stage], order[stage + 1 :]))
        self.waves[2].sort(key=lambda one: one[1].bit_count())
        self.t_each = -(-n_aa * self.rows[-1] // self.group)
        self.moves = PARTS * (n_aa // 2 - 1 + n_aa // 2)


class Exchange:
    def __init__(self, plan, source, target, send, recv, place):
        self.plan, self.source, self.target = plan, source, target
        self.send, self.recv, self.place, self.keys = send, recv, place, {}

    def copy(self, part, mask, bit):
        index = self.keys.setdefault((part, mask, bit), len(self.keys))
        aa, col = self.place
        return pltpu.make_async_remote_copy(
            src_ref=self.source(part, mask),
            dst_ref=self.target(part, mask),
            send_sem=self.send.at[index],
            recv_sem=self.recv.at[index],
            device_id=(aa ^ bit, col),
            device_id_type=MESH,
        )

    def own(self, first=0, last=None):
        for stage in range(len(self.plan.far))[first:last]:
            for part, order in enumerate(self.plan.orders):
                self.copy(part, 0, order[stage]).start()
        if first == 0:
            for part in range(PARTS):
                self.copy(part, 0, 1).start()

    def wave(self, which):
        for part, mask, bit, later in self.plan.waves[which]:
            self.copy(part, mask ^ bit, bit).wait_recv()
            for further in later:
                self.copy(part, mask, further).start()
            self.copy(part, mask, 1).start()

    def core(self, mask):
        for part in range(PARTS):
            self.copy(part, mask ^ 1, 1).wait_recv()

    def finish(self):
        for key in list(self.keys):
            self.copy(*key).wait_send()


def kernel(plan, fit_ac, fit_bd, amplitudes, sums, bd_all, t_all, *refs):
    count = len(plan.phases)
    highs, lows8, highs8 = refs[:count], refs[count : 2 * count], refs[2 * count : 3 * count]
    acc, t_high, t_low, blocks_a, stage, turned, t_stage, made, ready = refs[3 * count : 3 * count + 9]
    a_sem, own_sem, stage_sem, t_sem, z_send, z_recv, x_send, x_recv, r_send, r_recv, r_own = refs[3 * count + 9 :]
    aa, col = lax.axis_index("aa").astype(jnp.int32), lax.axis_index("col").astype(jnp.int32)
    n_col, n_aa = plan.n_col, plan.n_aa
    q_local, depth, d_local = plan.q_local, plan.depth, plan.d_local
    half = plan.columns // PARTS

    barrier = pltpu.get_barrier_semaphore()
    peers = [(aa, col ^ step) for step in range(1, n_col)] + [(aa ^ bit, col) for bit in [1] + plan.far]
    for peer in peers:
        pl.semaphore_signal(barrier, inc=1, device_id=peer, device_id_type=MESH)

    mine = pl.ds(pl.multiple_of((aa * n_col + col) * q_local, q_local), q_local)
    take = pltpu.make_async_copy(fit_bd, stage.at[0, pl.ds(0, q_local)], own_sem.at[0])
    take.start()
    keep = pltpu.make_async_copy(amplitudes, t_all.at[:, pl.ds(aa * d_local, d_local)], own_sem.at[1])
    keep.start()
    pl.semaphore_wait(barrier, len(peers))

    along = []
    for step in range(1, n_col):
        along.append(
            pltpu.make_async_remote_copy(
                src_ref=fit_bd,
                dst_ref=bd_all.at[mine],
                send_sem=z_send.at[step - 1],
                recv_sem=z_recv.at[step - 1],
                device_id=(aa, col ^ step),
                device_id_type=MESH,
            )
        )
        if step < plan.near:
            along[-1].start()
    take.wait()
    put = pltpu.make_async_copy(stage.at[0, pl.ds(0, q_local)], bd_all.at[mine], own_sem.at[0])
    put.start()

    def first_q(mask, rel):
        return pl.multiple_of(((aa ^ mask) * n_col + ((col // plan.near) ^ rel) * plan.near) * q_local, depth)

    def bd_piece(rel, part, mask):
        return bd_all.at[pl.ds(first_q(mask, rel), depth), pl.ds(part * half, half)]

    def t_piece(part, mask):
        return t_all.at[part, pl.ds((aa ^ mask) * d_local, d_local)]

    def t_source(part, mask):
        return amplitudes.at[part] if mask == 0 else t_piece(part, mask)

    place = (aa, col)
    exchanges = []
    for rel in range(plan.halves):
        piece = functools.partial(bd_piece, rel)
        exchanges.append(Exchange(plan, piece, piece, x_send.at[rel], x_recv.at[rel], place))
    exchange_t = Exchange(plan, t_source, t_piece, x_send.at[plan.halves], x_recv.at[plan.halves], place)

    def begin_half(rel):
        for step in range(max(1, rel * plan.near), (rel + 1) * plan.near):
            along[step - 1].wait_recv()
        if rel == 0:
            for step in range(plan.near, n_col):
                along[step - 1].start()
            put.wait()
        exchanges[rel].own()

    last = len(plan.phases) - 1
    events = [(0, 4, lambda: exchanges[0].wave(0)), (0, 7, lambda: exchange_t.own(0, 1))]
    events.append((1, -1, lambda: exchanges[0].wave(1)))
    events.append((1, 0, lambda: exchanges[0].wave(2)))
    for rel in range(1, plan.halves):
        events.append((1, 2, functools.partial(begin_half, rel)))
        events.append((1, 6, functools.partial(exchanges[rel].wave, 0)))
    events.append((1, 6, lambda: exchange_t.own(1)))
    events.append((1, 6, lambda: exchange_t.wave(0)))
    for rel in range(1, plan.halves):
        events.append((2, 0, functools.partial(exchanges[rel].wave, 1)))
        events.append((2, 2, functools.partial(exchanges[rel].wave, 2)))
    events.append((2, 5, lambda: exchange_t.wave(1)))

    def run_events(phase, at):
        for when, step, act in events:
            if when == phase and step == at:
                act()

    def loads(phase, index, slot):
        rows = plan.rows[phase]
        found = []
        for at, (mask, rel) in enumerate(plan.phases[phase]):
            found.append(
                pltpu.make_async_copy(
                    fit_ac.at[pl.ds(index * rows, rows), :, pl.ds(first_q(mask, rel), depth)],
                    blocks_a.at[slot, at % 4, pl.ds(at // 4 * rows, rows)],
                    a_sem.at[slot, at],
                )
            )
        return found

    def fetch(phase, index, slot):
        for one in loads(phase, index, slot):
            one.start()

    def bring(phase, at):
        pieces = plan.phases[phase]
        row = jnp.int32(0)
        for one, (mask, rel) in enumerate(pieces):
            row = jnp.where(at == one, first_q(mask, rel), row)
        slot = lax.rem(at, 2)
        return pltpu.make_async_copy(
            bd_all.at[pl.ds(pl.multiple_of(row, depth), depth)], stage.at[slot], stage_sem.at[slot]
        )

    def start_bring(phase, at):
        pieces = plan.phases[phase]
        for one, (mask, rel) in enumerate(pieces):
            if mask & 1:
                pl.when(at == one)(functools.partial(exchanges[rel].core, mask))

        @pl.when(at < len(pieces))
        def _():
            bring(phase, at).start()

    def arrange(phase, at):
        turned[...] = stage[lax.rem(at, 2)].T
        lanes = pl.ds(pl.multiple_of(at * depth, depth), depth)
        for k in range(plan.blocks):
            for d in range(0, plan.d_size, 2):
                first = k * plan.b_size * plan.d_size + d
                value = jnp.concatenate(
                    [turned[pl.ds(first + one, plan.b_size, stride=plan.d_size), :] for one in range(2)], axis=0
                )
                top, rest = split(value)
                to = (pl.ds((k * plan.d_size + d) * plan.b_size, 2 * plan.b_size), lanes)
                highs[phase][to] = (top.astype(F32) * SCALE).astype(BF16)
                lows8[phase][to] = (rest * B_LO).astype(F8)
                highs8[phase][to] = (value * B_HI).astype(F8)

    def prepare(phase):
        start_bring(phase, jnp.int32(0))
        start_bring(phase, jnp.int32(1))

        @pl.loop(0, len(plan.phases[phase]))
        def _(at):
            bring(phase, at).wait()
            arrange(phase, at)
            start_bring(phase, at + 2)

    dot = functools.partial(lax.dot_general, dimension_numbers=NT, preferred_element_type=F32)

    def multiply(phase, index):
        pieces, rows = plan.phases[phase], plan.rows[phase]
        slot = lax.rem(index, 2)
        for one in loads(phase, index, slot):
            one.wait()
        parts = [
            blocks_a[slot, at % 4, at // 4 * rows : at // 4 * rows + rows].reshape(rows * plan.c_local, depth)
            for at in range(len(pieces))
        ]
        value = jnp.concatenate(parts, axis=1)
        top, rest = split(value)
        made_here = dot(highs[phase][...], top)
        made_here += dot(lows8[phase][...], (value * A_HI).astype(F8))
        made_here += dot(highs8[phase][...], (rest * A_LO).astype(F8))
        count = plan.blocks * plan.d_size
        for row in range(rows):
            one = made_here[:, row * plan.c_local : (row + 1) * plan.c_local]
            one = one.reshape(count, plan.b_size, plan.c_local)
            at = index * rows + row
            if phase == 0:
                acc[:, at] = one
            else:
                acc[:, at] += one

    begin_half(0)
    fetch(0, 0, 0)
    prepared = False
    for phase in range(last):
        run_events(phase, -1)
        if not prepared:
            prepare(phase)
        steps, ahead = plan.a_local // plan.rows[phase], len(plan.phases[phase + 1])
        prepared = phase > 0 and ahead < steps
        plain_steps = steps - ahead if prepared else steps

        def before(index, low, high, phase=phase, steps=steps):
            @pl.when(index + 1 < steps)
            def _():
                fetch(phase, index + 1, lax.rem(index + 1, 2))

            @pl.when(index + 1 == steps)
            def _():
                fetch(phase + 1, 0, steps % 2)

            for at in range(low, high):
                if any(when == phase and step == at for when, step, _ in events):
                    pl.when(index == at)(functools.partial(run_events, phase, at))

        @pl.loop(0, plain_steps)
        def _(index, phase=phase, before=before, plain_steps=plain_steps):
            before(index, 0, plain_steps)
            multiply(phase, index)

        if prepared:
            start_bring(phase + 1, jnp.int32(0))

            @pl.loop(plain_steps, steps)
            def _(index, phase=phase, before=before, plain_steps=plain_steps, steps=steps):
                before(index, plain_steps, steps)
                at = index - plain_steps
                bring(phase + 1, at).wait()
                start_bring(phase + 1, at + 1)
                multiply(phase, index)
                arrange(phase + 1, at)

        for at in range(steps, 8):
            run_events(phase, at)

    for at in range(-1, 8):
        run_events(last, at)
    if not prepared:
        prepare(last)
    span = d_local * plan.c_local

    each = plan.t_each

    def t_copy(k, mask):
        slot = lax.rem(mask, 2 * each)
        src = t_all.at[k, pl.ds((aa ^ mask) * d_local, d_local)]
        return pltpu.make_async_copy(src, t_stage.at[slot], t_sem.at[slot])

    def t_arrange(k, mask):
        value = t_stage[lax.rem(mask, 2 * each)].reshape(span, plan.pairs) * UNDO
        top, rest = split(value)
        to = (k, pl.ds(pl.multiple_of((aa ^ mask) * span, span), span))
        t_high[to] = top
        t_low[to] = rest.astype(BF16)

    def t_begin(k, at):
        for one in range(each):
            t_copy(k, at * each + one).start()

    def t_end(k, at):
        for one in range(each):
            t_copy(k, at * each + one).wait()

    def t_work(k, at):
        for one in range(each):
            t_arrange(k, at * each + one)

    def t_gather(masks):
        for mask in masks:
            if mask & 1:
                exchange_t.core(mask)

    group, rows = plan.group, plan.rows[last]
    inner = group // rows
    plain = functools.partial(jnp.dot, preferred_element_type=F32)
    wide = 8 if plan.c_local % LANES == 0 else 1

    def ladder(k, start, size):
        total = None
        for d in range(0, plan.d_size, wide):
            parts = []
            for one in range(d, d + wide):
                part = acc[k * plan.d_size + one, pl.ds(start, size)]
                parts.append(part.reshape(size * plan.b_size, plan.c_local))
            x_high, x_low = split(jnp.concatenate(parts, axis=1) if wide > 1 else parts[0])
            at = slice(d * plan.c_local, (d + wide) * plan.c_local)
            t_top, t_rest = t_high[k, at], t_low[k, at]
            term = plain(x_high, t_top) + plain(x_low.astype(BF16), t_top) + plain(x_high, t_rest)
            total = term if total is None else total + term
        return total

    def away(start, size, number, k, step):
        to = col ^ step
        slot = lax.rem(number, 2)
        src = ready.at[slot, k, pl.ds(to * plan.b_out, plan.b_out), pl.ds(0, size)]
        dst = sums.at[step, k, :, pl.ds(start, size)]
        at = number * plan.blocks + k
        if step == 0:
            return pltpu.make_async_copy(src, dst, r_own.at[at])
        return pltpu.make_async_remote_copy(
            src_ref=src,
            dst_ref=dst,
            send_sem=r_send.at[at, step - 1],
            recv_sem=r_recv.at[at, step - 1],
            device_id=(aa, to),
            device_id_type=MESH,
        )

    total_steps = plan.a_local // rows

    def contract(index):
        @pl.when(index + 1 < total_steps)
        def _():
            fetch(last, index + 1, lax.rem(index + 1, 2))

        multiply(last, index)

    def left(start, size, number):
        for k in range(plan.blocks):
            away(start, size, number, k, 0).wait()
            for step in range(1, n_col):
                away(start, size, number, k, step).wait_send()

    def finish(start, size, number, first=None):
        slot = lax.rem(number, 2)

        @pl.loop(0, plan.blocks)
        def _(k):
            if first is not None:
                pl.when(jnp.logical_and(number == 0, k == 1))(first)
            total = ladder(k, start, size)
            for at in range(0, plan.pairs, LANES):
                made[0 : size * plan.b_size] = total[:, at : at + LANES]
                for b in range(plan.b_size):
                    ready[slot, k, b, 0:size, at : at + LANES] = made[pl.ds(b, size, stride=plan.b_size), :]
            for step in range(1, n_col):
                away(start, size, number, k, step).start()
            away(start, size, number, k, 0).start()

    if last < 2:
        exchange_t.wave(0)
        exchange_t.wave(1)
    keep.wait()
    early = each * (inner - 1)
    late = not any((mask & ~1).bit_count() > 1 for mask in range(early))
    if not late:
        exchange_t.wave(2)
        early = n_aa
    t_gather(range(early))
    t_begin(0, 0)

    @pl.loop(0, inner)
    def _(index):
        if late:

            @pl.when(index == inner - 2)
            def _():
                exchange_t.wave(2)
                t_gather(range(early, n_aa))

        @pl.when(index + 1 < inner)
        def _():
            t_begin(0, index + 1)

        t_end(0, index)

        @pl.when(index + 1 < total_steps)
        def _():
            fetch(last, index + 1, lax.rem(index + 1, 2))

        multiply(last, index)
        t_work(0, index)

    t_begin(1, 0)

    def t_second():
        @pl.loop(0, inner)
        def _(index):
            @pl.when(index + 1 < inner)
            def _():
                t_begin(1, index + 1)

            t_end(1, index)
            t_work(1, index)

    bulk = plan.a_local // group - 1

    @pl.loop(0, bulk)
    def _(which):
        @pl.when(which > 0)
        def _():
            @pl.loop(0, inner)
            def _(sub):
                contract(which * inner + sub)

        @pl.when(which >= 2)
        def _():
            left(pl.multiple_of((which - 2) * group, group), group, which - 2)

        finish(pl.multiple_of(which * group, group), group, which, t_second)

    tail, tail_inner = plan.tail, plan.tail // rows
    sent = [(which * group, group, jnp.int32(which)) for which in range(bulk)]
    sent += [(bulk * group + at * tail, tail, jnp.int32(bulk + at)) for at in range(2)]
    for at in range(2):

        @pl.loop(0, tail_inner)
        def _(sub, at=at):
            contract(bulk * inner + at * tail_inner + sub)

        if bulk + at >= 2:
            left(*sent[bulk + at - 2])
        finish(*sent[bulk + at])

    for one in sent[-2:]:
        left(*one)
    for one in along:
        one.wait_send()
    for one in exchanges + [exchange_t]:
        one.finish()
    for start, size, number in sent:
        for k in range(plan.blocks):
            for step in range(1, n_col):
                away(start, size, number, k, step).wait_recv()


def shards(n_aa, n_col, fit_ac, fit_bd, amplitudes):
    plan = Plan(n_aa, n_col, fit_ac, fit_bd, amplitudes)
    columns, count_q, c_local, pairs = plan.columns, plan.count_q, plan.c_local, plan.pairs
    dma, any_ = pltpu.SemaphoreType.DMA, pl.BlockSpec(memory_space=pl.ANY)
    sends = (plan.a_local // plan.group + 1) * plan.blocks
    widths = [plan.depth * len(phase) for phase in plan.phases]
    most = max(len(phase) for phase in plan.phases)
    sums, _, _ = pl.pallas_call(
        functools.partial(kernel, plan),
        in_specs=[any_] * 3,
        out_specs=[any_] * 3,
        out_shape=[
            jax.ShapeDtypeStruct((n_col, plan.blocks, plan.b_out, plan.a_local, pairs), F32),
            jax.ShapeDtypeStruct((count_q, columns), F32),
            jax.ShapeDtypeStruct((plan.blocks, plan.d_size, c_local, pairs), F32),
        ],
        scratch_shapes=[pltpu.VMEM((columns, width), BF16) for width in widths]
        + [pltpu.VMEM((columns, width), F8) for width in widths * 2]
        + [
            pltpu.VMEM((plan.blocks * plan.d_size, plan.a_local, plan.b_size, c_local), F32),
            pltpu.VMEM((plan.blocks, plan.d_size * c_local, pairs), BF16),
            pltpu.VMEM((plan.blocks, plan.d_size * c_local, pairs), BF16),
            pltpu.VMEM((2, 4, 8, c_local, plan.depth), F32),
            pltpu.VMEM((2, plan.depth, columns), F32),
            pltpu.VMEM((columns, plan.depth), F32),
            pltpu.VMEM((2 * plan.t_each, plan.d_local, c_local, pairs), F32),
            pltpu.VMEM((plan.group * plan.b_size, LANES), F32),
            pltpu.VMEM((2, plan.blocks, plan.b_size, plan.group, pairs), F32),
            dma((2, most)),
            dma((2,)),
            dma((2,)),
            dma((2 * plan.t_each,)),
            dma((n_col - 1,)),
            dma((n_col - 1,)),
            dma((plan.halves + 1, plan.moves)),
            dma((plan.halves + 1, plan.moves)),
            dma((sends, n_col - 1)),
            dma((sends, n_col - 1)),
            dma((sends,)),
        ],
        compiler_params=pltpu.CompilerParams(vmem_limit_bytes=VMEM_LIMIT, collective_id=0, has_side_effects=True),
    )(fit_ac, fit_bd, amplitudes)
    return sums.sum(axis=0)


def solution(mesh):
    placed = (P("aa", "col", None), P(("aa", "col"), None), P(None, "aa", "col", None))
    body = functools.partial(shards, mesh.shape["aa"], mesh.shape["col"])
    return jax.shard_map(
        body, mesh=mesh, in_specs=placed, out_specs=P(None, "col", "aa", None), check_vma=False
    )
```
